32 devices in a mesh: tp: 8 (over y, x, core), dp: 4 (over z).
Axes of the slice: x: 2, y: 2, z: 4, core: 2. Of those that a mesh axis runs over, the one named last changes fastest.
Arguments:
- activations: bfloat16 [64, 512, 4096], P('dp', None, 'tp'), may hold values from -6 to 6
- query_output_cotangent: bfloat16 [64, 512, 4096], P('dp', None, 'tp'), may hold values from -6 to 6
- value_output_cotangent: bfloat16 [64, 512, 4096], P('dp', None, 'tp'), may hold values from -6 to 6
- lengths: int32 [64], P('dp'), may hold values from 1 to 512
- reducing_matrices_pair: bfloat16 [2, 4096, 128], P(None, 'tp'), may hold values from -0.09375 to 0.09375
- expanding_matrices_pair: bfloat16 [2, 128, 4096], P(None, None, 'tp'), may hold values from -0.5 to 0.5
- width_side_projections: bfloat16 [2, 4096, 128], P(None, 'tp'), may hold values from -0.09375 to 0.09375
- narrow_random_sketch: bfloat16 [128, 16], replicated, may hold values from -0.5 to 0.5
- projected_first_moment: float32 [8192], replicated, may hold values from -6 to 6
- projected_second_moment: float32 [8192], replicated, may hold values from 0.1 to 10
- targets: bfloat16 [1024, 8192], P('dp', 'tp'), may hold values from -6 to 6
Outputs:
- scores: float32 [64, 1024], P('dp', 'tp')
The draws below stay inside these ranges and needn't reach their ends.
All inputs are finite; a program needn't handle non-finite values.
Results may differ from the reference program's by a relative error of at most 0.023.
Values may be sent and summed in bfloat16 or wider, within the bound.
A program may use at most 128 MiB of HBM per device.

```python
import math
import jax
import jax.numpy as jnp
from jax import lax

HIDDEN_SIZE = 4096
LOW_DIMENSION = 128
KD = 128
SKETCH_LOW_COORD = 16
SEQ = 512
EVAL_CASES = 1024
K = 8192
DSH = 512
WIN = 64
N_TP = 8


def with_ends(values, rng, least, top_value):
    spot = [jax.random.randint(jax.random.fold_in(rng, axis), (), 0, length) for axis, length in enumerate(values.shape)]
    widest = values.shape.index(max(values.shape))
    neighbour = spot[:widest] + [(spot[widest] + 1) % values.shape[widest]] + spot[widest + 1:]
    return values.at[tuple(spot)].set(least).at[tuple(neighbour)].set(top_value)


def steps_of(key, shape, cuts, least, largest):
    gain, own = 1.0, jax.random.fold_in(key, 6)
    for dim, blocks in cuts:
        heights = jnp.exp(jax.random.uniform(jax.random.fold_in(own, dim), (blocks,), jnp.float32, least / len(cuts), largest / len(cuts)))
        gain = gain * jnp.repeat(heights, shape[dim] // blocks).reshape([-1 if axis == dim else 1 for axis in range(len(shape))])
    return gain


def noise(key, extent, deviation, most, split=(), held_as=jnp.bfloat16):
    result = deviation * jax.random.normal(key, extent, jnp.float32)
    if split:
        result = result * steps_of(key, extent, split, -0.22, 0.18)
    return jnp.clip(result, -most, most).astype(held_as)


def setup_inputs(seed: int = 0) -> dict:
    key_list = jax.random.split(jax.random.key(seed), 12)
    return {
        "activations": noise(key_list[0], (WIN, SEQ, HIDDEN_SIZE), 1.0, 6.0, ((0, 4), (2, 8))),
        "query_output_cotangent": noise(key_list[1], (WIN, SEQ, HIDDEN_SIZE), 1.0, 6.0, ((0, 4), (2, 8))),
        "value_output_cotangent": noise(key_list[2], (WIN, SEQ, HIDDEN_SIZE), 1.0, 6.0, ((0, 4), (2, 8))),
        "lengths": with_ends(jax.random.randint(key_list[3], (WIN,), 1, SEQ + 1), jax.random.fold_in(key_list[3], 1), 1, SEQ).astype(jnp.int32),
        "reducing_matrices_pair": noise(key_list[4], (2, HIDDEN_SIZE, LOW_DIMENSION), HIDDEN_SIZE ** -0.5, 0.09375, ((1, 8),)),
        "expanding_matrices_pair": noise(key_list[5], (2, LOW_DIMENSION, HIDDEN_SIZE), LOW_DIMENSION ** -0.5, 0.5, ((2, 8),)),
        "width_side_projections": noise(key_list[6], (2, HIDDEN_SIZE, KD), HIDDEN_SIZE ** -0.5, 0.09375, ((1, 8),)),
        "narrow_random_sketch": noise(key_list[7], (LOW_DIMENSION, SKETCH_LOW_COORD), LOW_DIMENSION ** -0.5, 0.5),
        "projected_first_moment": noise(key_list[8], (K,), 1.0, 6.0, (), jnp.float32),
        "projected_second_moment": jnp.clip(jnp.exp(jax.random.uniform(key_list[9], (K,), jnp.float32, math.log(0.1), math.log(10.0))), 0.1, 10.0),
        "targets": noise(key_list[10], (EVAL_CASES, K), 1.0, 6.0, ((0, 4), (1, 8))),
    }


def compute_features(token_sums, token_mask, layout, rank_cols):
    wide_cols = (token_sums.shape[-1] - 4 * rank_cols) // 3
    bounds = [0, rank_cols, 2 * rank_cols, 2 * rank_cols + wide_cols, 3 * rank_cols + wide_cols, 3 * rank_cols + 2 * wide_cols, 4 * rank_cols + 2 * wide_cols, 4 * rank_cols + 3 * wide_cols]
    pieces = [token_sums[..., bounds[i]:bounds[i + 1]] for i in range(7)]
    down_q, down_v, input_side, back_q, output_q, back_v, output_v = pieces
    weights = token_mask[..., None]
    pattern = layout + 'r,' + layout + 'k->erk'

    def outer_sum(left_side, right_side):
        return jnp.einsum(pattern, left_side, right_side, precision=lax.Precision.HIGHEST)
    stacked = jnp.stack([outer_sum(back_q * weights, input_side), outer_sum(back_v * weights, input_side), outer_sum(down_q * weights, output_q), outer_sum(down_v * weights, output_v)], axis=1)
    return stacked.reshape(stacked.shape[0], -1)

def adam_update(features, first_moment, second_moment):
    mixed = 0.9 * first_moment + 0.1 * features
    spread = 0.999 * second_moment + 0.001 * features * features
    return mixed / (jnp.sqrt(spread) + 1e-08)

def combine_factors(reducing_matrices_pair, expanding_matrices_pair, narrow_random_sketch):
    attention_key_reducer = jnp.dot(reducing_matrices_pair[0], narrow_random_sketch, preferred_element_type=jnp.float32).astype(jnp.bfloat16)
    value_down_factor = jnp.dot(reducing_matrices_pair[1], narrow_random_sketch, preferred_element_type=jnp.float32).astype(jnp.bfloat16)
    query_up_factor = jnp.dot(expanding_matrices_pair[0].T, narrow_random_sketch, preferred_element_type=jnp.float32).astype(jnp.bfloat16)
    value_up_factor = jnp.dot(expanding_matrices_pair[1].T, narrow_random_sketch, preferred_element_type=jnp.float32).astype(jnp.bfloat16)
    return (attention_key_reducer, value_down_factor, query_up_factor, value_up_factor)

def reference(activations, query_output_cotangent, value_output_cotangent, lengths, reducing_matrices_pair, expanding_matrices_pair, width_side_projections, narrow_random_sketch, projected_first_moment, projected_second_moment, targets):
    attention_key_reducer, value_down_factor, query_up_factor, value_up_factor = combine_factors(reducing_matrices_pair, expanding_matrices_pair, narrow_random_sketch)
    rank_cols = narrow_random_sketch.shape[1]
    w_left = jnp.concatenate([attention_key_reducer, value_down_factor, width_side_projections[0]], axis=1)
    w_query = jnp.concatenate([query_up_factor, width_side_projections[1]], axis=1)
    w_value = jnp.concatenate([value_up_factor, width_side_projections[1]], axis=1)
    left_groups = w_left.astype(jnp.float32).reshape(N_TP, DSH, -1)
    query_groups = w_query.astype(jnp.float32).reshape(N_TP, DSH, -1)
    value_groups = w_value.astype(jnp.float32).reshape(N_TP, DSH, -1)

    def grouped(rows, weights):
        split_rows = rows.astype(jnp.float32).reshape(SEQ, N_TP, DSH)
        parts = jnp.einsum('sgd,gdc->gsc', split_rows, weights, precision=lax.Precision.HIGHEST)
        rounded = lax.optimization_barrier(parts.astype(jnp.bfloat16)).astype(jnp.float32)
        return lax.optimization_barrier(jnp.sum(rounded, axis=0))

    def one_example(items):
        rows_x, rows_q, rows_v, length = items
        token_sums = jnp.concatenate([grouped(rows_x, left_groups), grouped(rows_q, query_groups), grouped(rows_v, value_groups)], axis=-1)
        token_mask = (jnp.arange(SEQ, dtype=jnp.int32) < length).astype(jnp.float32)
        return compute_features(token_sums[None], token_mask[None], 'es', rank_cols)[0]
    features = lax.map(one_example, (activations, query_output_cotangent, value_output_cotangent, lengths))
    update = adam_update(features, projected_first_moment, projected_second_moment)
    train_rows = (update * lax.rsqrt(lax.optimization_barrier(jnp.sum(update * update, axis=1)) + 1e-06)[:, None]).astype(jnp.bfloat16)
    target_float = targets.astype(jnp.float32)
    unit_targets = (target_float * lax.rsqrt(lax.optimization_barrier(jnp.sum(target_float * target_float, axis=1)) + 1e-06)[:, None]).astype(jnp.bfloat16)
    scores = jnp.dot(train_rows, unit_targets.T, preferred_element_type=jnp.float32)
    return scores * math.sqrt(K)
```

```python
import math

import jax
import jax.numpy as jnp
from jax import lax
from jax.sharding import PartitionSpec as P


def adam_update(features, first_moment, second_moment):
    mixed = 0.9 * first_moment + 0.1 * features
    spread = 0.999 * second_moment + 0.001 * features * features
    return mixed / (jnp.sqrt(spread) + 1e-08)


def combine_factors(reducing_matrices_pair, expanding_matrices_pair, narrow_random_sketch):
    attention_key_reducer = jnp.dot(
        reducing_matrices_pair[0], narrow_random_sketch, preferred_element_type=jnp.float32
    ).astype(jnp.bfloat16)
    value_down_factor = jnp.dot(
        reducing_matrices_pair[1], narrow_random_sketch, preferred_element_type=jnp.float32
    ).astype(jnp.bfloat16)
    query_up_factor = jnp.dot(
        expanding_matrices_pair[0].T, narrow_random_sketch, preferred_element_type=jnp.float32
    ).astype(jnp.bfloat16)
    value_up_factor = jnp.dot(
        expanding_matrices_pair[1].T, narrow_random_sketch, preferred_element_type=jnp.float32
    ).astype(jnp.bfloat16)
    return (attention_key_reducer, value_down_factor, query_up_factor, value_up_factor)


def body(
    activations,
    query_output_cotangent,
    value_output_cotangent,
    lengths,
    reducing_matrices_pair,
    expanding_matrices_pair,
    width_side_projections,
    narrow_random_sketch,
    projected_first_moment,
    projected_second_moment,
    targets,
):
    attention_key_reducer, value_down_factor, query_up_factor, value_up_factor = combine_factors(
        reducing_matrices_pair, expanding_matrices_pair, narrow_random_sketch
    )
    rank_cols = narrow_random_sketch.shape[1]
    w_left = jnp.concatenate(
        [attention_key_reducer, value_down_factor, width_side_projections[0]], axis=1
    )
    w_query = jnp.concatenate([query_up_factor, width_side_projections[1]], axis=1)
    w_value = jnp.concatenate([value_up_factor, width_side_projections[1]], axis=1)
    groups = lax.axis_size("tp")
    parts = lax.axis_size("dp")
    member = lax.axis_index("tp")
    local_ex, seq_len = activations.shape[:2]
    feature_count = projected_first_moment.shape[0]
    positions = jnp.arange(seq_len, dtype=jnp.int32)
    token_mask = (positions[None, :] < lengths[:, None])[..., None]

    def project(rows, weights):
        out = jnp.einsum("esd,dc->esc", rows, weights, preferred_element_type=jnp.float32)
        return out.astype(jnp.bfloat16)

    left = project(activations, w_left)
    right_q = project(query_output_cotangent, w_query)
    right_v = project(value_output_cotangent, w_value)
    narrow = jnp.concatenate(
        [left[..., : 2 * rank_cols], right_q[..., :rank_cols], right_v[..., :rank_cols]], axis=-1
    )
    narrow = jnp.where(token_mask, narrow, jnp.zeros((), jnp.bfloat16))
    narrow = lax.psum(narrow, "tp")

    def outer_sum(first, wide):
        return jnp.einsum(
            "esr,esk->erk",
            narrow[..., first * rank_cols : (first + 1) * rank_cols],
            wide,
            preferred_element_type=jnp.float32,
        )

    own_features = jnp.concatenate(
        [
            outer_sum(2, left[..., 2 * rank_cols :]),
            outer_sum(3, left[..., 2 * rank_cols :]),
            outer_sum(0, right_q[..., rank_cols:]),
            outer_sum(1, right_v[..., rank_cols:]),
        ],
        axis=1,
    ).reshape(local_ex, -1)
    features = lax.psum_scatter(
        own_features.astype(jnp.bfloat16), "tp", scatter_dimension=1, tiled=True
    ).astype(jnp.float32)
    span = feature_count // groups
    first_moment = lax.dynamic_slice_in_dim(projected_first_moment, member * span, span)
    second_moment = lax.dynamic_slice_in_dim(projected_second_moment, member * span, span)
    update = adam_update(features, first_moment, second_moment).astype(jnp.bfloat16)
    update = lax.all_gather(update, "dp", axis=0, tiled=True)
    wide_update = update.astype(jnp.float32)
    target_float = targets.astype(jnp.float32)
    update_sq = jnp.sum(wide_update * wide_update, axis=1)
    target_sq = jnp.sum(target_float * target_float, axis=1)
    dots = lax.dot_general(
        update, targets, (((1,), (1,)), ((), ())), preferred_element_type=jnp.float32
    )
    rows = jnp.concatenate(
        [dots, jnp.broadcast_to(update_sq[:, None], (dots.shape[0], 128))], axis=1
    ).reshape(parts, local_ex, -1)
    extra = jnp.pad(target_sq, (0, 128))
    rows = jnp.concatenate([rows, jnp.broadcast_to(extra, (parts, 8, extra.shape[0]))], axis=1)
    rows = lax.psum(rows, "tp")
    rows = lax.all_to_all(rows, "dp", split_axis=0, concat_axis=0, tiled=True)
    owned = targets.shape[0]
    totals = jnp.moveaxis(rows[:, :, :owned], 0, 1).reshape(local_ex + 8, parts * owned)
    columns = parts * owned // groups
    totals = lax.dynamic_slice_in_dim(totals, member * columns, columns, 1)
    row_scale = lax.rsqrt(rows[0, :local_ex, owned : owned + 1] + 1e-06)
    column_scale = lax.rsqrt(totals[local_ex : local_ex + 1] + 1e-06)
    return totals[:local_ex] * row_scale * column_scale * math.sqrt(feature_count)


def solution(mesh):
    placed = (
        P("dp", None, "tp"),
        P("dp", None, "tp"),
        P("dp", None, "tp"),
        P("dp"),
        P(None, "tp", None),
        P(None, None, "tp"),
        P(None, "tp", None),
        P(),
        P(),
        P(),
        P("dp", "tp"),
    )
    return jax.shard_map(body, mesh=mesh, in_specs=placed, out_specs=P("dp", "tp"), check_vma=False)
```

```python
import functools
import math

import jax
import jax.numpy as jnp
from jax import lax
from jax.experimental import pallas as pl
from jax.experimental.pallas import tpu as pltpu
from jax.sharding import PartitionSpec as P

MESH = pl.DeviceIdType.MESH
F32 = jnp.float32
BF16 = jnp.bfloat16
BATCHES = 2


def mm(a, b, ca=1, cb=0):
    return lax.dot_general(a, b, (((ca,), (cb,)), ((), ())), preferred_element_type=F32)


def kernel(
    nd,
    n,
    x_hbm,
    q_hbm,
    v_hbm,
    len_ref,
    red_ref,
    exp_ref,
    width_ref,
    sketch_ref,
    m1_ref,
    m2_ref,
    t_hbm,
    out_ref,
    x_buf,
    q_buf,
    v_buf,
    t_buf,
    w_buf,
    wide,
    pair_out,
    pair_in,
    mine,
    comb,
    rs_in,
    gath,
    feat_out,
    feat_in,
    upd,
    u_all,
    sq_out,
    sq_in,
    t_out,
    t_in,
    g_out,
    g_in,
    load_sem,
    t_sem,
    pair_s,
    pair_r,
    rs_s,
    rs_r,
    ag_s,
    ag_r,
    fwd_s,
    fwd_r,
    feat_s,
    feat_r,
    u_s,
    u_r,
    sq_s,
    sq_r,
    tn_s,
    tn_r,
    g_s,
    g_r,
):
    d = lax.axis_index("dp")
    c = lax.axis_index("tp")
    chips = n // 2
    chip, core = c // 2, lax.rem(c, 2)
    partner = chip * 2 + 1 - core
    examples, seq, depth = x_buf.shape
    pairs = examples // 2
    ranks = gath.shape[2]
    rc = ranks // 4
    cut = seq // chips
    rows = ranks // n
    own_targets = t_buf.shape[0]
    out_cols = out_ref.shape[1]
    piece = min(own_targets, out_cols)
    halves = own_targets // piece
    slots = out_cols // piece
    per_batch = pairs // BATCHES

    def remote(src, dst, send, recv, dd, cc):
        return pltpu.make_async_remote_copy(
            src_ref=src, dst_ref=dst, send_sem=send, recv_sem=recv, device_id={"dp": dd, "tp": cc}, device_id_type=MESH
        )

    def load(e):
        return [
            pltpu.make_async_copy(src.at[e], dst.at[e], load_sem.at[j, e])
            for j, (src, dst) in enumerate(((x_hbm, x_buf), (q_hbm, q_buf), (v_hbm, v_buf)))
        ]

    def start_loads(i, _):
        for e in ((1 - core) * pairs + i, core * pairs + i):
            for copy in load(e):
                copy.start()
        return 0

    lax.fori_loop(0, pairs, start_loads, 0)
    t_copy = pltpu.make_async_copy(t_hbm, t_buf, t_sem)
    t_copy.start()

    barrier = pltpu.get_barrier_semaphore()
    total = nd * n
    me = d * n + c

    def greet(r, _):
        other = lax.rem(me + r, total)
        pl.semaphore_signal(
            barrier, inc=1, device_id={"dp": other // n, "tp": lax.rem(other, n)}, device_id_type=MESH
        )
        return 0

    lax.fori_loop(1, total, greet, 0)

    sketch = sketch_ref[...]

    def placed(slot):
        row = lax.broadcasted_iota(jnp.int32, (rc, 128), 0)
        col = lax.broadcasted_iota(jnp.int32, (rc, 128), 1)
        return mm(sketch, jnp.where(col == row + slot * rc, 1.0, 0.0).astype(BF16)).astype(BF16)

    w_buf[0, :, :128] = (mm(red_ref[0], placed(2)) + mm(red_ref[1], placed(3))).astype(BF16)
    w_buf[1, :, :128] = mm(exp_ref[0], placed(0), 0, 0).astype(BF16)
    w_buf[2, :, :128] = mm(exp_ref[1], placed(1), 0, 0).astype(BF16)
    w_buf[0, :, 128:] = width_ref[0]
    w_buf[1, :, 128:] = width_ref[1]
    w_buf[2, :, 128:] = width_ref[1]

    pl.semaphore_wait(barrier, total - 1)

    def project(e, out, i):
        for copy in load(e):
            copy.wait()
        narrow = None
        for j, buf in enumerate((x_buf, q_buf, v_buf)):
            res = mm(buf[e], w_buf[j])
            wide[e, :, j * 128 : (j + 1) * 128] = res[:, 128:].astype(BF16)
            narrow = res[:, :128] if narrow is None else narrow + res[:, :128]
        flat = narrow.T[:ranks]
        token = lax.broadcasted_iota(jnp.int32, (ranks, seq), 1)
        flat = jnp.where(token < len_ref[e], flat, 0.0).astype(BF16)
        for q in range(chips):
            out[i, q] = flat[:, q * cut : (q + 1) * cut]

    def pair_copy(i):
        return remote(pair_out.at[i], pair_in.at[i], pair_s.at[i], pair_r.at[i], d, partner)

    def rs_copy(i, r):
        to = lax.rem(chip + r, chips)
        return remote(comb.at[i, to], rs_in.at[i, r], rs_s.at[i, r], rs_r.at[i, r], d, to * 2 + core)

    def ag_copy(i, r, place):
        to = lax.rem(chip + r, chips)
        block = gath.at[core * pairs + i, place]
        return remote(block, block, ag_s.at[i, r], ag_r.at[i, r], d, to * 2 + core)

    def fwd_copy(i, side):
        block = gath.at[side * pairs + i]
        return remote(block, block, fwd_s.at[i], fwd_r.at[i], d, partner)

    def feat_copy(b, r):
        to = lax.rem(c + r, n)
        return remote(feat_out.at[b, to], feat_in.at[b, r], feat_s.at[b, r], feat_r.at[b, r], d, to)

    def home(h):
        return (d * own_targets + h * piece) // out_cols, lax.rem(d * own_targets + h * piece, out_cols) // piece

    def t_copy_out(i, h):
        j, s = home(h)
        return remote(t_out.at[h], t_in.at[s, c], tn_s.at[i, h], tn_r.at[s, c], i, j)

    def g_copy(i, h):
        j, s = home(h)
        return remote(g_out.at[i, h], g_in.at[s, c], g_s.at[i, h], g_r.at[s, c], i, j)

    def scatter_pieces(make, own_in, own_out):
        for i in range(nd):
            for h in range(halves):
                j, s = home(h)
                here = jnp.logical_and(d == i, c == j)

                @pl.when(jnp.logical_not(here))
                def _():
                    make(i, h).start()

                @pl.when(here)
                def _():
                    own_in[s, c] = own_out(i, h)

    def drain_pieces(make):
        for i in range(nd):
            for h in range(halves):
                j, _ = home(h)

                @pl.when(jnp.logical_not(jnp.logical_and(d == i, c == j)))
                def _():
                    make(i, h).wait_send()

    def receive_pieces(buf, send, recv):
        for s in range(slots):
            source = (c * out_cols + s * piece) // own_targets
            for cc in range(n):

                @pl.when(jnp.logical_not(jnp.logical_and(d == source, c == cc)))
                def _():
                    block = buf.at[s, cc]
                    remote(block, block, send.at[0, 0], recv.at[s, cc], source, cc).wait_recv()

    def step(it, _):
        @pl.when(it < pairs)
        def _():
            project((1 - core) * pairs + it, pair_out, it)
            pair_copy(it).start()
            project(core * pairs + it, mine, it)

        @pl.when(jnp.logical_and(it >= 1, it < pairs + 1))
        def _():
            i = it - 1
            pair_copy(i).wait_recv()
            comb[i] = (mine[i].astype(F32) + pair_in[i].astype(F32)).astype(BF16)
            for r in range(1, chips):
                rs_copy(i, r).start()

        @pl.when(jnp.logical_and(it >= 2, it < pairs + 2))
        def _():
            i = it - 2
            whole = comb[i, chip].astype(F32)
            for r in range(1, chips):
                rs_copy(i, r).wait_recv()
                whole = whole + rs_in[i, r].astype(F32)
            gath[core * pairs + i, chip] = whole.astype(BF16)
            for r in range(1, chips):
                ag_copy(i, r, chip).start()

        @pl.when(jnp.logical_and(it >= 3, it < pairs + 3))
        def _():
            i = it - 3
            for r in range(1, chips):
                ag_copy(i, r, lax.rem(chip + chips - r, chips)).wait_recv()
            fwd_copy(i, core).start()

        @pl.when(it >= 4)
        def _():
            i = it - 4
            fwd_copy(i, 1 - core).wait_recv()
            found = []
            for e in (i, pairs + i):
                g = jnp.concatenate([gath[e, q] for q in range(chips)], axis=1)
                found.append(
                    jnp.concatenate(
                        [
                            mm(g[: 2 * rc], wide[e, :, :128]),
                            mm(g[2 * rc : 3 * rc], wide[e, :, 128:256]),
                            mm(g[3 * rc :], wide[e, :, 256:]),
                        ],
                        axis=0,
                    )
                )
            b, place = i // per_batch, lax.rem(i, per_batch)
            for q in range(n):
                feat_out[b, q, place] = jnp.concatenate(
                    [f[q * rows : (q + 1) * rows] for f in found], axis=0
                ).astype(BF16)

            @pl.when(place == per_batch - 1)
            def _():
                for r in range(1, n):
                    feat_copy(b, r).start()

        @pl.when(it == pairs)
        def _():
            t_copy.wait()
            t = t_buf[...].astype(F32)
            norm = jnp.broadcast_to(jnp.sum(t * t, axis=1, keepdims=True), (own_targets, 128)).T
            for h in range(halves):
                t_out[h] = norm[:8, h * piece : (h + 1) * piece]
            scatter_pieces(t_copy_out, t_in, lambda i, h: t_out[h])

        return 0

    lax.fori_loop(0, pairs + 4, step, 0)

    m1, m2 = m1_ref[c], m2_ref[c]
    for b in range(BATCHES):
        f = feat_out[b, c].astype(F32)
        for r in range(1, n):
            feat_copy(b, r).wait_recv()
            f = f + feat_in[b, r].astype(F32)
        for h in range(2):
            fh = f[:, h * rows : (h + 1) * rows]
            new = (0.9 * m1 + 0.1 * fh) / (jnp.sqrt(0.999 * m2 + 0.001 * fh * fh) + 1e-08)
            upd[h, b * per_batch : (b + 1) * per_batch] = new
    squares = None
    for r in range(rows):
        u = jnp.concatenate([upd[0, :, r, :], upd[1, :, r, :]], axis=0).astype(BF16)
        u_all[d, r] = u
        wide_u = u.astype(F32)
        squares = wide_u * wide_u if squares is None else squares + wide_u * wide_u

    def u_copy(r, place):
        to = lax.rem(d + r, nd)
        return remote(u_all.at[place], u_all.at[place], u_s.at[r], u_r.at[r], to, c)

    def sq_copy(r):
        to = lax.rem(c + r, n)
        return remote(sq_out, sq_in.at[r], sq_s.at[r], sq_r.at[r], d, to)

    for r in range(1, nd):
        u_copy(r, d).start()
    sq_out[...] = squares
    for r in range(1, n):
        sq_copy(r).start()
    for r in range(1, nd):
        u_copy(r, lax.rem(d + nd - r, nd)).wait_recv()
    u_rows = jnp.concatenate(
        [jnp.concatenate([u_all[i, r] for r in range(rows)], axis=1) for i in range(nd)], axis=0
    )
    dots = mm(u_rows, t_buf[...], 1, 1).astype(BF16)
    for i in range(nd):
        for h in range(halves):
            g_out[i, h] = dots[i * examples : (i + 1) * examples, h * piece : (h + 1) * piece]
    scatter_pieces(g_copy, g_in, lambda i, h: g_out[i, h])

    for r in range(1, n):
        sq_copy(r).wait_recv()
        squares = squares + sq_in[r]
    row_scale = lax.rsqrt(jnp.sum(squares, axis=1, keepdims=True) + 1e-06) * math.sqrt(ranks * 128)
    receive_pieces(t_in, tn_s, tn_r)
    column_scale = []
    for s in range(slots):
        norm = t_in[s, 0]
        for cc in range(1, n):
            norm = norm + t_in[s, cc]
        column_scale.append(lax.rsqrt(norm[:1] + 1e-06))
    receive_pieces(g_in, g_s, g_r)
    for s in range(slots):
        acc = g_in[s, 0].astype(F32)
        for cc in range(1, n):
            acc = acc + g_in[s, cc].astype(F32)
        out_ref[:, s * piece : (s + 1) * piece] = acc * row_scale * column_scale[s]

    def drain(i, _):
        pair_copy(i).wait_send()
        fwd_copy(i, core).wait_send()
        for r in range(1, chips):
            rs_copy(i, r).wait_send()
            ag_copy(i, r, chip).wait_send()
        return 0

    lax.fori_loop(0, pairs, drain, 0)
    for r in range(1, n):
        for b in range(BATCHES):
            feat_copy(b, r).wait_send()
        sq_copy(r).wait_send()
    for r in range(1, nd):
        u_copy(r, d).wait_send()
    drain_pieces(t_copy_out)
    drain_pieces(g_copy)


def body(nd, n, x, q, v, lengths, reducing, expanding, width, sketch, m1, m2, targets):
    examples, seq, depth = x.shape
    ranks = 4 * sketch.shape[1]
    pairs, chips, rows = examples // 2, n // 2, ranks // n
    cut = seq // chips
    own_targets = targets.shape[0]
    out_cols = own_targets * nd // n
    piece = min(own_targets, out_cols)
    halves, slots = own_targets // piece, out_cols // piece
    dma = pltpu.SemaphoreType.DMA
    anywhere = pl.BlockSpec(memory_space=pl.ANY)
    vmem = pl.BlockSpec(memory_space=pltpu.VMEM)
    smem = pl.BlockSpec(memory_space=pltpu.SMEM)
    per_batch = pairs // BATCHES
    return pl.pallas_call(
        functools.partial(kernel, nd, n),
        out_shape=jax.ShapeDtypeStruct((examples, out_cols), F32),
        in_specs=[anywhere] * 3 + [smem] + [vmem] * 6 + [anywhere],
        out_specs=vmem,
        scratch_shapes=[
            pltpu.VMEM((examples, seq, depth), BF16),
            pltpu.VMEM((examples, seq, depth), BF16),
            pltpu.VMEM((examples, seq, depth), BF16),
            pltpu.VMEM(targets.shape, BF16),
            pltpu.VMEM((3, depth, 256), BF16),
            pltpu.VMEM((examples, seq, 384), BF16),
            pltpu.VMEM((pairs, chips, ranks, cut), BF16),
            pltpu.VMEM((pairs, chips, ranks, cut), BF16),
            pltpu.VMEM((pairs, chips, ranks, cut), BF16),
            pltpu.VMEM((pairs, chips, ranks, cut), BF16),
            pltpu.VMEM((pairs, chips, ranks, cut), BF16),
            pltpu.VMEM((examples, chips, ranks, cut), BF16),
            pltpu.VMEM((BATCHES, n, per_batch, 2 * rows, 128), BF16),
            pltpu.VMEM((BATCHES, n, per_batch, 2 * rows, 128), BF16),
            pltpu.VMEM((2, pairs, rows, 128), F32),
            pltpu.VMEM((nd, rows, examples, 128), BF16),
            pltpu.VMEM((examples, 128), F32),
            pltpu.VMEM((n, examples, 128), F32),
            pltpu.VMEM((halves, 8, piece), F32),
            pltpu.VMEM((slots, n, 8, piece), F32),
            pltpu.VMEM((nd, halves, examples, piece), BF16),
            pltpu.VMEM((slots, n, examples, piece), BF16),
            dma((3, examples)),
            dma,
            dma((pairs,)),
            dma((pairs,)),
            dma((pairs, chips)),
            dma((pairs, chips)),
            dma((pairs, chips)),
            dma((pairs, chips)),
            dma((pairs,)),
            dma((pairs,)),
            dma((BATCHES, n)),
            dma((BATCHES, n)),
            dma((nd,)),
            dma((nd,)),
            dma((n,)),
            dma((n,)),
            dma((nd, halves)),
            dma((slots, n)),
            dma((nd, halves)),
            dma((slots, n)),
        ],
        compiler_params=pltpu.CompilerParams(
            collective_id=0, has_side_effects=True, vmem_limit_bytes=56 * 1024 * 1024
        ),
    )(
        x,
        q,
        v,
        lengths,
        reducing,
        expanding,
        width,
        sketch,
        m1.reshape(n, rows, 128),
        m2.reshape(n, rows, 128),
        targets,
    )


def solution(mesh):
    placed = (
        P("dp", None, "tp"),
        P("dp", None, "tp"),
        P("dp", None, "tp"),
        P("dp"),
        P(None, "tp", None),
        P(None, None, "tp"),
        P(None, "tp", None),
        P(),
        P(),
        P(),
        P("dp", "tp"),
    )
    names = mesh.axis_names
    order = (mesh.shape["dp"], mesh.shape["tp"])
    run = functools.partial(body, *order)
    assert set(names) == {"dp", "tp"}
    return jax.shard_map(run, mesh=mesh, in_specs=placed, out_specs=P("dp", "tp"), check_vma=False)
```

```python
import functools
import math

import jax
import jax.numpy as jnp
from jax import lax
from jax.experimental import pallas as pl
from jax.experimental.pallas import tpu as pltpu
from jax.sharding import PartitionSpec as P

MESH = pl.DeviceIdType.MESH
F32 = jnp.float32
BF16 = jnp.bfloat16
BATCHES = 2


def mm(a, b, ca=1, cb=0):
    return lax.dot_general(a, b, (((ca,), (cb,)), ((), ())), preferred_element_type=F32)


def kernel(
    nd,
    n,
    x_hbm,
    q_hbm,
    v_hbm,
    len_ref,
    red_hbm,
    exp_hbm,
    width_hbm,
    sketch_ref,
    m1_ref,
    m2_ref,
    t_hbm,
    out_ref,
    x_buf,
    q_buf,
    v_buf,
    t_buf,
    red_ref,
    exp_ref,
    width_ref,
    w_buf,
    wide,
    pair_out,
    pair_in,
    mine,
    comb,
    rs_in,
    gath,
    feat_out,
    feat_in,
    upd,
    u_all,
    sq_out,
    sq_in,
    t_out,
    t_in,
    g_out,
    g_in,
    load_sem,
    t_sem,
    fixed_sem,
    pair_s,
    pair_r,
    rs_s,
    rs_r,
    ag_s,
    ag_r,
    fwd_s,
    fwd_r,
    feat_s,
    feat_r,
    u_s,
    u_r,
    sq_s,
    sq_r,
    tn_s,
    tn_r,
    g_s,
    g_r,
):
    d = lax.axis_index("dp")
    c = lax.axis_index("tp")
    chips = n // 2
    chip, core = c // 2, lax.rem(c, 2)
    partner = chip * 2 + 1 - core
    examples, seq, depth = x_buf.shape
    pairs = examples // 2
    rc = sketch_ref.shape[0]
    ranks = 4 * rc
    half = seq // 2
    rows = ranks // n
    own_targets = t_buf.shape[0]
    out_cols = out_ref.shape[1]
    piece = min(own_targets, out_cols)
    halves = own_targets // piece
    slots = out_cols // piece
    per_batch = pairs // BATCHES

    def remote(src, dst, send, recv, dd, cc):
        return pltpu.make_async_remote_copy(
            src_ref=src, dst_ref=dst, send_sem=send, recv_sem=recv, device_id={"dp": dd, "tp": cc}, device_id_type=MESH
        )

    def load(e):
        return [
            pltpu.make_async_copy(src.at[e], dst.at[e], load_sem.at[j, e])
            for j, (src, dst) in enumerate(((x_hbm, x_buf), (q_hbm, q_buf), (v_hbm, v_buf)))
        ]

    def start_loads(i, _):
        for e in ((1 - core) * pairs + i, core * pairs + i):
            for copy in load(e):
                copy.start()
        return 0

    fixed = [
        pltpu.make_async_copy(src, dst, fixed_sem.at[j])
        for j, (src, dst) in enumerate(((red_hbm, red_ref), (exp_hbm, exp_ref), (width_hbm, width_ref)))
    ]
    for copy in fixed:
        copy.start()
    lax.fori_loop(0, pairs, start_loads, 0)
    t_copy = pltpu.make_async_copy(t_hbm, t_buf, t_sem)
    t_copy.start()

    barrier = pltpu.get_barrier_semaphore()
    total = nd * n
    me = d * n + c

    def greet(r, _):
        other = lax.rem(me + r, total)
        pl.semaphore_signal(
            barrier, inc=1, device_id={"dp": other // n, "tp": lax.rem(other, n)}, device_id_type=MESH
        )
        return 0

    lax.fori_loop(1, total, greet, 0)

    sketch = sketch_ref[...]
    for copy in fixed:
        copy.wait()

    def placed(slot):
        row = lax.broadcasted_iota(jnp.int32, (rc, 128), 0)
        col = lax.broadcasted_iota(jnp.int32, (rc, 128), 1)
        here = jnp.logical_or(col == row + slot * rc, col == row + slot * rc + ranks)
        return mm(sketch, jnp.where(here, 1.0, 0.0).astype(BF16), 0, 0).astype(BF16)

    w_buf[0, :, :128] = (mm(red_ref[0], placed(2)) + mm(red_ref[1], placed(3))).astype(BF16)
    w_buf[1, :, :128] = mm(exp_ref[0], placed(0), 0, 0).astype(BF16)
    w_buf[2, :, :128] = mm(exp_ref[1], placed(1), 0, 0).astype(BF16)
    w_buf[0, :, 128:] = width_ref[0]
    w_buf[1, :, 128:] = width_ref[1]
    w_buf[2, :, 128:] = width_ref[1]

    pl.semaphore_wait(barrier, total - 1)

    def project(e, out, i):
        for copy in load(e):
            copy.wait()
        row = lax.broadcasted_iota(jnp.int32, (half, 128), 0)
        upper = lax.broadcasted_iota(jnp.int32, (half, 128), 1) >= ranks
        live = jnp.where(upper, row + half, row) < len_ref[e]
        for k in range(half // 128):
            sums = []
            for late in range(2):
                span = pl.ds(late * half + k * 128, 128)
                narrow = None
                for j, buf in enumerate((x_buf, q_buf, v_buf)):
                    res = mm(buf[e, span], w_buf[j])
                    wide[e, span, j * 128 : (j + 1) * 128] = res[:, 128:].astype(BF16)
                    narrow = res[:, :128] if narrow is None else narrow + res[:, :128]
                sums.append(narrow)
            packed = jnp.where(upper[:128], sums[1], sums[0])
            packed = jnp.where(live[k * 128 : (k + 1) * 128], packed, 0.0).astype(BF16)
            out[i, :, :, k * 128 : (k + 1) * 128] = packed.T.reshape(chips, 128 // chips, 128)

    def pair_copy(i):
        return remote(pair_out.at[i], pair_in.at[i], pair_s.at[i], pair_r.at[i], d, partner)

    def rs_copy(i, r):
        to = lax.rem(chip + r, chips)
        return remote(comb.at[i, to], rs_in.at[i, r], rs_s.at[i, r], rs_r.at[i, r], d, to * 2 + core)

    def ag_copy(i, r, place):
        to = lax.rem(chip + r, chips)
        block = gath.at[core * pairs + i, place]
        return remote(block, block, ag_s.at[i, r], ag_r.at[i, r], d, to * 2 + core)

    def fwd_copy(i, side):
        block = gath.at[side * pairs + i]
        return remote(block, block, fwd_s.at[i], fwd_r.at[i], d, partner)

    def feat_copy(b, r):
        to = lax.rem(c + r, n)
        return remote(feat_out.at[b, to], feat_in.at[b, r], feat_s.at[b, r], feat_r.at[b, r], d, to)

    def home(h):
        return (d * own_targets + h * piece) // out_cols, lax.rem(d * own_targets + h * piece, out_cols) // piece

    def t_copy_out(i, h):
        j, s = home(h)
        return remote(t_out.at[h], t_in.at[s, c], tn_s.at[i, h], tn_r.at[s, c], i, j)

    def g_copy(i, h):
        j, s = home(h)
        return remote(g_out.at[i, h], g_in.at[s, c], g_s.at[i, h], g_r.at[s, c], i, j)

    def scatter_pieces(make, own_in, own_out):
        for i in range(nd):
            for h in range(halves):
                j, s = home(h)
                here = jnp.logical_and(d == i, c == j)

                @pl.when(jnp.logical_not(here))
                def _():
                    make(i, h).start()

                @pl.when(here)
                def _():
                    own_in[s, c] = own_out(i, h)

    def drain_pieces(make):
        for i in range(nd):
            for h in range(halves):
                j, _ = home(h)

                @pl.when(jnp.logical_not(jnp.logical_and(d == i, c == j)))
                def _():
                    make(i, h).wait_send()

    def receive_pieces(buf, send, recv):
        for s in range(slots):
            source = (c * out_cols + s * piece) // own_targets
            for cc in range(n):

                @pl.when(jnp.logical_not(jnp.logical_and(d == source, c == cc)))
                def _():
                    block = buf.at[s, cc]
                    remote(block, block, send.at[0, 0], recv.at[s, cc], source, cc).wait_recv()

    def step(it, _):
        @pl.when(it < pairs)
        def _():
            project((1 - core) * pairs + it, pair_out, it)
            pair_copy(it).start()
            project(core * pairs + it, mine, it)

        @pl.when(jnp.logical_and(it >= 1, it < pairs + 1))
        def _():
            i = it - 1
            pair_copy(i).wait_recv()
            comb[i] = (mine[i].astype(F32) + pair_in[i].astype(F32)).astype(BF16)
            for r in range(1, chips):
                rs_copy(i, r).start()

        @pl.when(jnp.logical_and(it >= 2, it < pairs + 2))
        def _():
            i = it - 2
            whole = comb[i, chip].astype(F32)
            for r in range(1, chips):
                rs_copy(i, r).wait_recv()
                whole = whole + rs_in[i, r].astype(F32)
            gath[core * pairs + i, chip] = whole.astype(BF16)
            for r in range(1, chips):
                ag_copy(i, r, chip).start()

        @pl.when(jnp.logical_and(it >= 3, it < pairs + 3))
        def _():
            i = it - 3
            for r in range(1, chips):
                ag_copy(i, r, lax.rem(chip + chips - r, chips)).wait_recv()
            fwd_copy(i, core).start()

        @pl.when(it >= 4)
        def _():
            i = it - 4
            fwd_copy(i, 1 - core).wait_recv()
            found = []
            for e in (i, pairs + i):
                g = gath[e].reshape(128, half)
                g = jnp.concatenate([g[:ranks], g[ranks:]], axis=1)
                left = mm(g, wide[e, :, :256])
                found.append(
                    jnp.concatenate(
                        [
                            left[: 2 * rc, :128],
                            left[2 * rc : 3 * rc, 128:],
                            mm(g[3 * rc :], wide[e, :, 256:]),
                        ],
                        axis=0,
                    )
                )
            b, place = i // per_batch, lax.rem(i, per_batch)
            for q in range(n):
                feat_out[b, q, place] = jnp.concatenate(
                    [f[q * rows : (q + 1) * rows] for f in found], axis=0
                ).astype(BF16)

            @pl.when(place == per_batch - 1)
            def _():
                for r in range(1, n):
                    feat_copy(b, r).start()

        @pl.when(it == pairs)
        def _():
            t_copy.wait()
            t = t_buf[...].astype(F32)
            norm = jnp.broadcast_to(jnp.sum(t * t, axis=1, keepdims=True), (own_targets, 128)).T
            for h in range(halves):
                t_out[h] = norm[:8, h * piece : (h + 1) * piece]
            scatter_pieces(t_copy_out, t_in, lambda i, h: t_out[h])

        return 0

    lax.fori_loop(0, pairs + 4, step, 0)

    m1, m2 = m1_ref[c], m2_ref[c]
    for b in range(BATCHES):
        f = feat_out[b, c].astype(F32)
        for r in range(1, n):
            feat_copy(b, r).wait_recv()
            f = f + feat_in[b, r].astype(F32)
        for h in range(2):
            fh = f[:, h * rows : (h + 1) * rows]
            new = (0.9 * m1 + 0.1 * fh) / (jnp.sqrt(0.999 * m2 + 0.001 * fh * fh) + 1e-08)
            upd[h, b * per_batch : (b + 1) * per_batch] = new
    squares = None
    for r in range(rows):
        u = jnp.concatenate([upd[0, :, r, :], upd[1, :, r, :]], axis=0).astype(BF16)
        u_all[d, r] = u
        wide_u = u.astype(F32)
        squares = wide_u * wide_u if squares is None else squares + wide_u * wide_u

    def u_copy(r, place):
        to = lax.rem(d + r, nd)
        return remote(u_all.at[place], u_all.at[place], u_s.at[r], u_r.at[r], to, c)

    def sq_copy(r):
        to = lax.rem(c + r, n)
        return remote(sq_out, sq_in.at[r], sq_s.at[r], sq_r.at[r], d, to)

    for r in range(1, nd):
        u_copy(r, d).start()
    sq_out[...] = squares
    for r in range(1, n):
        sq_copy(r).start()
    for r in range(1, nd):
        u_copy(r, lax.rem(d + nd - r, nd)).wait_recv()
    u_rows = jnp.concatenate(
        [jnp.concatenate([u_all[i, r] for r in range(rows)], axis=1) for i in range(nd)], axis=0
    )
    dots = mm(u_rows, t_buf[...], 1, 1).astype(BF16)
    for i in range(nd):
        for h in range(halves):
            g_out[i, h] = dots[i * examples : (i + 1) * examples, h * piece : (h + 1) * piece]
    scatter_pieces(g_copy, g_in, lambda i, h: g_out[i, h])

    for r in range(1, n):
        sq_copy(r).wait_recv()
        squares = squares + sq_in[r]
    row_scale = lax.rsqrt(jnp.sum(squares, axis=1, keepdims=True) + 1e-06) * math.sqrt(ranks * 128)
    receive_pieces(t_in, tn_s, tn_r)
    column_scale = []
    for s in range(slots):
        norm = t_in[s, 0]
        for cc in range(1, n):
            norm = norm + t_in[s, cc]
        column_scale.append(lax.rsqrt(norm[:1] + 1e-06))
    receive_pieces(g_in, g_s, g_r)
    for s in range(slots):
        acc = g_in[s, 0].astype(F32)
        for cc in range(1, n):
            acc = acc + g_in[s, cc].astype(F32)
        out_ref[:, s * piece : (s + 1) * piece] = acc * row_scale * column_scale[s]

    def drain(i, _):
        pair_copy(i).wait_send()
        fwd_copy(i, core).wait_send()
        for r in range(1, chips):
            rs_copy(i, r).wait_send()
            ag_copy(i, r, chip).wait_send()
        return 0

    lax.fori_loop(0, pairs, drain, 0)
    for r in range(1, n):
        for b in range(BATCHES):
            feat_copy(b, r).wait_send()
        sq_copy(r).wait_send()
    for r in range(1, nd):
        u_copy(r, d).wait_send()
    drain_pieces(t_copy_out)
    drain_pieces(g_copy)


def body(nd, n, x, q, v, lengths, reducing, expanding, width, sketch, m1, m2, targets):
    examples, seq, depth = x.shape
    ranks = 4 * sketch.shape[1]
    pairs, chips, rows = examples // 2, n // 2, ranks // n
    own_targets = targets.shape[0]
    out_cols = own_targets * nd // n
    piece = min(own_targets, out_cols)
    halves, slots = own_targets // piece, out_cols // piece
    dma = pltpu.SemaphoreType.DMA
    anywhere = pl.BlockSpec(memory_space=pl.ANY)
    vmem = pl.BlockSpec(memory_space=pltpu.VMEM)
    smem = pl.BlockSpec(memory_space=pltpu.SMEM)
    per_batch = pairs // BATCHES
    return pl.pallas_call(
        functools.partial(kernel, nd, n),
        out_shape=jax.ShapeDtypeStruct((examples, out_cols), F32),
        in_specs=[anywhere] * 3 + [smem] + [anywhere] * 3 + [vmem] * 3 + [anywhere],
        out_specs=vmem,
        scratch_shapes=[
            pltpu.VMEM((examples, seq, depth), BF16),
            pltpu.VMEM((examples, seq, depth), BF16),
            pltpu.VMEM((examples, seq, depth), BF16),
            pltpu.VMEM(targets.shape, BF16),
            pltpu.VMEM(reducing.shape, BF16),
            pltpu.VMEM(expanding.shape, BF16),
            pltpu.VMEM(width.shape, BF16),
            pltpu.VMEM((3, depth, 256), BF16),
            pltpu.VMEM((examples, seq, 384), BF16),
            pltpu.VMEM((pairs, chips, 128 // chips, seq // 2), BF16),
            pltpu.VMEM((pairs, chips, 128 // chips, seq // 2), BF16),
            pltpu.VMEM((pairs, chips, 128 // chips, seq // 2), BF16),
            pltpu.VMEM((pairs, chips, 128 // chips, seq // 2), BF16),
            pltpu.VMEM((pairs, chips, 128 // chips, seq // 2), BF16),
            pltpu.VMEM((examples, chips, 128 // chips, seq // 2), BF16),
            pltpu.VMEM((BATCHES, n, per_batch, 2 * rows, 128), BF16),
            pltpu.VMEM((BATCHES, n, per_batch, 2 * rows, 128), BF16),
            pltpu.VMEM((2, pairs, rows, 128), F32),
            pltpu.VMEM((nd, rows, examples, 128), BF16),
            pltpu.VMEM((examples, 128), F32),
            pltpu.VMEM((n, examples, 128), F32),
            pltpu.VMEM((halves, 8, piece), F32),
            pltpu.VMEM((slots, n, 8, piece), F32),
            pltpu.VMEM((nd, halves, examples, piece), BF16),
            pltpu.VMEM((slots, n, examples, piece), BF16),
            dma((3, examples)),
            dma,
            dma((3,)),
            dma((pairs,)),
            dma((pairs,)),
            dma((pairs, chips)),
            dma((pairs, chips)),
            dma((pairs, chips)),
            dma((pairs, chips)),
            dma((pairs,)),
            dma((pairs,)),
            dma((BATCHES, n)),
            dma((BATCHES, n)),
            dma((nd,)),
            dma((nd,)),
            dma((n,)),
            dma((n,)),
            dma((nd, halves)),
            dma((slots, n)),
            dma((nd, halves)),
            dma((slots, n)),
        ],
        compiler_params=pltpu.CompilerParams(
            collective_id=0, has_side_effects=True, vmem_limit_bytes=56 * 1024 * 1024
        ),
    )(
        x,
        q,
        v,
        lengths,
        reducing,
        expanding,
        width,
        sketch.T,
        m1.reshape(n, rows, 128),
        m2.reshape(n, rows, 128),
        targets,
    )


def solution(mesh):
    placed = (
        P("dp", None, "tp"),
        P("dp", None, "tp"),
        P("dp", None, "tp"),
        P("dp"),
        P(None, "tp", None),
        P(None, None, "tp"),
        P(None, "tp", None),
        P(),
        P(),
        P(),
        P("dp", "tp"),
    )
    names = mesh.axis_names
    order = (mesh.shape["dp"], mesh.shape["tp"])
    run = functools.partial(body, *order)
    assert set(names) == {"dp", "tp"}
    return jax.shard_map(run, mesh=mesh, in_specs=placed, out_specs=P("dp", "tp"), check_vma=False)
```
